32 devices in a mesh: groups: 2 (over y), tiles: 4 (over z), freq: 2 (over x), field: 2 (over core).
Axes of the slice: x: 2, y: 2, z: 4, core: 2. Of those that a mesh axis runs over, the one named last changes fastest.
Arguments:
- fields: bfloat16 [2, 4, 512, 1024], P('field', 'tiles', ('groups', 'freq')), parts along dimension 2, may hold values from -7.5 to 7.5
- slot_tile_ids: int32 [4], replicated, may hold values from 0 to 3, each once
- neighbour_tile_ids: int32 [4, 4], replicated, may hold values from 0 to 3
- neighbour_rotation_code: int32 [4, 4], replicated, may hold values from 0 to 7
- paired_tile_ids: int32 [4, 2], P('tiles'), may hold values from 0 to 3
Outputs:
- csd: float32 [8, 2, 2, 32, 128, 128], P(('groups', 'tiles'), None, None, ('freq', 'field')), parts along dimension 0
The draws below stay inside these ranges and needn't reach their ends.
There are 2 independent parts, one for each index of `groups`. The reference program is written for one: setup_inputs(seed, part) draws one part's arguments, and reference() takes and returns one part's arrays. A program takes and returns all parts, laid end to end along the dimension named above; an argument that names none is the same for every part. Nothing has to cross between parts.
All inputs are finite; a program needn't handle non-finite values.
Results may differ from the reference program's by a relative error of at most 0.0095.
Values may be sent and summed in bfloat16 or wider, within the bound.
A program may use at most 64 MiB of HBM per device.

```python
import math
import jax
import jax.numpy as jnp
from jax import lax

SIDE = 32
PARTNERS_EACH = 2
SEGLEN = 64
SMOOTH = 2
SLOT_COUNT = 4
SEGS = 4
TIME_SAMPLES = 256
TILE_CELLS = 1024


def draw_fields(key, part):
    leading = (2, SLOT_COUNT, TIME_SAMPLES, 1)
    streams = jax.random.split(jax.random.fold_in(key, 17), 4)
    cell_index = jnp.arange(TILE_CELLS, dtype=jnp.int32)
    row_index = cell_index // SIDE
    col_index = cell_index % SIDE
    row_sign = (1 - 2 * (row_index % 2)).astype(jnp.float32)
    col_sign = (1 - 2 * (col_index % 2)).astype(jnp.float32)
    row_cos = jnp.where(row_index % 2 == 0, 1 - row_index % 4, 0).astype(jnp.float32)
    row_sin = jnp.where(row_index % 2 == 1, 2 - row_index % 4, 0).astype(jnp.float32)
    col_cos = jnp.where(col_index % 2 == 0, 1 - col_index % 4, 0).astype(jnp.float32)
    col_sin = jnp.where(col_index % 2 == 1, 2 - col_index % 4, 0).astype(jnp.float32)
    wave_shape = (2, SLOT_COUNT, TIME_SAMPLES, 4)
    jitter_shape = (2, SLOT_COUNT, TIME_SAMPLES, TILE_CELLS)
    row_amp = 1.2 * jax.random.truncated_normal(streams[0], -1.7, 1.7, leading, jnp.float32)
    col_amp = 1.2 * jax.random.truncated_normal(streams[1], -1.7, 1.7, leading, jnp.float32)
    wave_amp = jax.random.truncated_normal(streams[2], -1.7, 1.7, wave_shape, jnp.float32)
    jitter_part = 0.35 * jax.random.truncated_normal(streams[3], -3.0, 3.0, jitter_shape, jnp.float32)
    wave_part = wave_amp[..., 0:1] * (row_cos * col_cos) + wave_amp[..., 1:2] * (row_cos * col_sin)
    wave_part = wave_part + wave_amp[..., 2:3] * (row_sin * col_cos) + wave_amp[..., 3:4] * (row_sin * col_sin)
    values = row_amp * row_sign + col_amp * col_sign + wave_part + jitter_part
    return values.astype(jnp.bfloat16)


def place_ends(array, own_key, low, largest):
    longest = array.shape.index(max(array.shape))
    spots = []
    for shift in (0, 1):
        where = [jax.random.randint(jax.random.fold_in(own_key, axis), (), 0, length) for axis, length in enumerate(array.shape)]
        where[longest] = (where[longest] + shift) % array.shape[longest]
        spots.append(tuple(where))
    return array.at[spots[0]].set(low).at[spots[1]].set(largest)


def setup_inputs(seed: int = 0, part: int = 0) -> dict:
    splits = jax.random.split(jax.random.key(seed), 6)
    part_keys = jax.random.split(jax.random.fold_in(splits[5], part), 6)
    return {
        "fields": draw_fields(jax.random.fold_in(jax.random.fold_in(splits[5], part), 71), part),
        "slot_tile_ids": jax.random.permutation(splits[1], SLOT_COUNT).astype(jnp.int32),
        "neighbour_tile_ids": place_ends(jax.random.randint(splits[2], (SLOT_COUNT, 4), 0, SLOT_COUNT), jax.random.fold_in(splits[2], 1), 0, SLOT_COUNT - 1).astype(jnp.int32),
        "neighbour_rotation_code": place_ends(jax.random.randint(splits[3], (SLOT_COUNT, 4), 0, 8), jax.random.fold_in(splits[3], 1), 0, 7).astype(jnp.int32),
        "paired_tile_ids": place_ends(jax.random.randint(splits[4], (SLOT_COUNT, PARTNERS_EACH), 0, SLOT_COUNT), jax.random.fold_in(splits[4], 1), 0, SLOT_COUNT - 1).astype(jnp.int32),
    }


diffusion = 0.25


def slot_lookup(slot_tile_ids, tile_ids):
    matches = (slot_tile_ids[None, :] == tile_ids.reshape(-1)[:, None]).astype(jnp.int32)
    positions = jnp.sum(matches * jnp.arange(slot_tile_ids.shape[0], dtype=jnp.int32)[None, :], axis=1)
    return positions.reshape(tile_ids.shape).astype(jnp.int32)


def tile_edges(field, tile_side):
    cell_count = field.shape[-1]
    north = field[..., :tile_side]
    east = field[..., tile_side - 1::tile_side]
    south = field[..., cell_count - tile_side:]
    west = field[..., ::tile_side]
    return jnp.stack([north, east, south, west], axis=-3)


def pick_rims(all_edges, near_slots, codes):
    chosen = all_edges[near_slots, codes % 4]
    flipped = chosen[..., ::-1]
    return jnp.where((codes // 4 == 1)[:, :, None, None], flipped, chosen)


def smooth_step(field, rims, tile_side):
    cell_count = field.shape[-1]
    values = field.astype(jnp.float32)
    edge_vals = rims.astype(jnp.float32)
    above_row = jnp.concatenate([edge_vals[:, 0], values[..., :cell_count - tile_side]], axis=-1)
    below_row = jnp.concatenate([values[..., tile_side:], edge_vals[:, 2]], axis=-1)
    column_pos = jnp.arange(cell_count, dtype=jnp.int32) % tile_side
    west_full = jnp.repeat(edge_vals[:, 3], tile_side, axis=-1)
    east_full = jnp.repeat(edge_vals[:, 1], tile_side, axis=-1)
    leftward = jnp.where(column_pos == 0, west_full, jnp.roll(values, 1, axis=-1))
    rightward = jnp.where(column_pos == tile_side - 1, east_full, jnp.roll(values, -1, axis=-1))
    laplace = above_row + below_row + leftward + rightward - 4.0 * values
    return (values + diffusion * laplace).astype(jnp.bfloat16)


def coarse_sums(field, tile_side):
    leading = field.shape[:-1]
    blocks = field.astype(jnp.float32).reshape(leading + (tile_side // 2, 2, tile_side // 4, 4))
    return jnp.sum(blocks, axis=(-3, -1)).reshape(leading + ((tile_side // 2) * (tile_side // 4),))


def window_table(seg_length):
    samples = jnp.arange(seg_length, dtype=jnp.int32)
    frequency = jnp.arange(seg_length // 2, dtype=jnp.int32)
    products = (frequency[:, None] * samples[None, :]) % seg_length
    angles = (2.0 * math.pi / seg_length) * products.astype(jnp.float32)
    window = 0.5 - 0.5 * jnp.cos((2.0 * math.pi / seg_length) * samples.astype(jnp.float32))
    dft_table = jnp.stack([window[None, :] * jnp.cos(angles), -window[None, :] * jnp.sin(angles)])
    return dft_table, jnp.sum(window * window)


def segment_spectra(coarse, dft_table):
    leading = coarse.shape[0]
    segments = coarse.reshape(leading, -1, dft_table.shape[-1], coarse.shape[-1])
    spectra = jnp.einsum("cft,nstp->nscfp", dft_table, segments, precision=lax.Precision.HIGHEST)
    return spectra.astype(jnp.bfloat16)


def reference(fields, slot_tile_ids, neighbour_tile_ids, neighbour_rotation_code, paired_tile_ids):
    near_slots = slot_lookup(slot_tile_ids, neighbour_tile_ids)
    partner_slots = slot_lookup(slot_tile_ids, paired_tile_ids)
    dft_table, window_power = window_table(SEGLEN)
    spectra = []
    for field_index in range(2):
        field = fields[field_index]
        for sweep_index in range(SMOOTH):
            rims = pick_rims(tile_edges(field, SIDE), near_slots, neighbour_rotation_code)
            field = smooth_step(field, rims, SIDE)
        spectra.append(segment_spectra(coarse_sums(field, SIDE), dft_table))
    height = spectra[0].astype(jnp.float32)
    partner = spectra[1][partner_slots].astype(jnp.float32)
    rotated = jnp.stack([height[:, :, 1], -height[:, :, 0]], axis=2)
    stacked = jnp.stack([height, rotated], axis=1)
    cross = jnp.einsum("noscfi,nkscfj->nkofij", stacked, partner, precision=lax.Precision.HIGHEST)
    return cross / (SEGS * window_power)
```

```python
import functools

import jax
import jax.numpy as jnp
import numpy as np
from jax import lax
from jax.experimental import pallas as pl
from jax.experimental.pallas import tpu as pltpu
from jax.sharding import PartitionSpec as P

SIDE = 32
SEGLEN = 64
CELLS = SIDE * SIDE
EDGE = 4 * SIDE
PAIRS = EDGE // 2
COARSE = CELLS // 8
MESH = pl.DeviceIdType.MESH


def smooth_cells(field, rims):
    padded = np.zeros(field.shape[:-2] + (SIDE + 2, SIDE + 2))
    padded[..., 1:-1, 1:-1] = field
    padded[..., 0, 1:-1] = rims[..., 0, :]
    padded[..., 1:-1, -1] = rims[..., 1, :]
    padded[..., -1, 1:-1] = rims[..., 2, :]
    padded[..., 1:-1, 0] = rims[..., 3, :]
    around = padded[..., :-2, 1:-1] + padded[..., 2:, 1:-1] + padded[..., 1:-1, :-2] + padded[..., 1:-1, 2:]
    return 0.25 * around


def coarse_cells(field):
    blocks = field.reshape(field.shape[:-2] + (SIDE // 2, 2, SIDE // 4, 4))
    return blocks.sum(axis=(-3, -1)).reshape(field.shape[:-2] + (COARSE,))


def edges_of(field):
    return np.stack([field[..., 0, :], field[..., :, -1], field[..., -1, :], field[..., :, 0]], axis=-2)


def edge_pairs(field):
    edges = edges_of(field)
    return edges.reshape(edges.shape[:-2] + (PAIRS, 2)).sum(axis=-1)


def spatial_tables():
    cells = np.eye(CELLS).reshape(CELLS, SIDE, SIDE)
    rims = np.eye(EDGE).reshape(EDGE, 4, SIDE)
    cell_zero = np.zeros((EDGE, SIDE, SIDE))
    rim_zero = np.zeros((CELLS, 4, SIDE))
    once = smooth_cells(cells, rim_zero)
    rim_once = smooth_cells(cell_zero, rims)
    own_coarse = coarse_cells(smooth_cells(once, rim_zero))
    outer = edges_of(cells).reshape(CELLS, EDGE)
    own_pairs = edge_pairs(once)
    sender = np.concatenate([own_coarse, outer, own_pairs, own_pairs], axis=1)
    rim_coarse = coarse_cells(smooth_cells(rim_once, np.zeros((EDGE, 4, SIDE)))).T
    rim_pairs = edge_pairs(rim_once).T
    pair_rims = np.repeat(np.eye(PAIRS), 2, axis=1).reshape(PAIRS, 4, SIDE)
    pair_coarse = coarse_cells(smooth_cells(np.zeros((PAIRS, SIDE, SIDE)), pair_rims)).T * 0.5
    pair_coarse = pair_coarse * 1.0
    flip = np.kron(np.eye(4), np.eye(SIDE)[::-1])
    pair_flip = np.kron(np.eye(4), np.eye(SIDE // 2)[::-1])
    both = np.concatenate([np.eye(EDGE), flip])
    pair_both = np.concatenate([np.eye(PAIRS), pair_flip])
    pair_own = np.concatenate([pair_both, pair_both], axis=1)
    pair_rim = pair_both @ rim_pairs
    pair_coarse = np.concatenate([pair_coarse, np.zeros((COARSE, EDGE - PAIRS))], axis=1)
    receiver = np.concatenate([both, pair_own, pair_rim, rim_coarse, pair_coarse, np.eye(COARSE)])
    return sender.astype(jnp.bfloat16), receiver.astype(jnp.bfloat16)


def hann():
    return 0.5 - 0.5 * np.cos(2.0 * np.pi * np.arange(SEGLEN) / SEGLEN)


def time_table(segments, bands):
    per_band = SEGLEN // 2 // bands
    window = hann()
    table = np.zeros((bands, 2, segments, per_band, segments, SEGLEN))
    for band in range(bands):
        for inner in range(per_band):
            angles = 2.0 * np.pi * (((band * per_band + inner) * np.arange(SEGLEN)) % SEGLEN) / SEGLEN
            for segment in range(segments):
                table[band, 0, segment, inner, segment] = window * np.cos(angles)
                table[band, 1, segment, inner, segment] = -window * np.sin(angles)
    return table.reshape(bands * 2 * segments * per_band, segments * SEGLEN).astype(np.float32)


def repeat(count, body):
    if count <= 4:
        for step in range(count):
            body(step)
    else:
        lax.fori_loop(0, count, lambda step, carry: (body(step), carry)[1], 0)


def exchange_kernel(nz, nf, rows, packed, field_ref, spatial_ref, time_ref, out_ref, send, send_sem, recv_sem, own_sem):
    group = lax.axis_index("groups")
    my_z = lax.axis_index("tiles")
    my_f = lax.axis_index("freq")
    my_c = lax.axis_index("field")
    last = send.shape[1]
    bands = 2 * nf

    def peers(dz, visit):
        z = lax.rem(my_z + dz, nz)
        for df in range(nf):
            for dc in range(2):
                yield_at = df * 2 + dc
                f = lax.rem(my_f + df, nf)
                c = lax.rem(my_c + dc, 2)
                visit(dz, yield_at, z, f, c)

    def each_peer(visit):
        def same(dz, where, z, f, c):
            if where:
                visit(True, dz, where, z, f, c)

        peers(0, same)
        repeat(nz - 1, lambda step: peers(step + 1, functools.partial(visit, False)))

    barrier = pltpu.get_barrier_semaphore()

    def greet(near, dz, where, z, f, c):
        pl.semaphore_signal(barrier, inc=1, device_id=(group, z, f, c), device_id_type=MESH)

    each_peer(greet)

    mapped = jnp.dot(field_ref[...], spatial_ref[...], preferred_element_type=jnp.float32)
    spectra = jnp.dot(
        time_ref[...], mapped, precision=lax.Precision.HIGHEST, preferred_element_type=jnp.float32
    )
    half = rows // 2
    lane = lax.broadcasted_iota(jnp.int32, (half, EDGE), 1)
    for band in range(bands):
        block = spectra[band * rows : (band + 1) * rows]
        send[band, 0:rows, :] = block[:, 0:COARSE].astype(jnp.bfloat16)
        send[band, rows : 2 * rows, :] = block[:, COARSE : COARSE + EDGE].astype(jnp.bfloat16)
        pairs = block[:, COARSE + EDGE :]
        if packed:
            pairs = jnp.where(lane < PAIRS, pairs[:half], pairs[half:])
        send[band, 2 * rows :, :] = pairs.astype(jnp.bfloat16)

    pl.semaphore_wait(barrier, nz * nf * 2 - 1)

    mine = my_c * nf + my_f

    def copy(first, dz, where, z, f, c, source_z, source):
        return pltpu.make_async_remote_copy(
            src_ref=send.at[f * 2 + c, pl.ds(first, last - first), :],
            dst_ref=out_ref.at[source_z, source, pl.ds(first, last - first), :],
            send_sem=send_sem.at[dz, where],
            recv_sem=recv_sem.at[source_z, source],
            device_id=(group, z, f, c),
            device_id_type=MESH,
        )

    def start(near, dz, where, z, f, c):
        if near:
            copy(0, dz, where, z, f, c, my_z, mine).start()
        else:
            @pl.when(my_c == 1)
            def _():
                copy(0, dz, where, z, f, c, my_z, mine).start()

            @pl.when(my_c == 0)
            def _():
                copy(rows, dz, where, z, f, c, my_z, mine).start()

    each_peer(start)
    own = pltpu.make_async_copy(send.at[my_f * 2 + my_c], out_ref.at[my_z, mine], own_sem)
    own.start()

    def finish(near, dz, where, z, f, c):
        if near:
            copy(0, dz, where, z, f, c, my_z, mine).wait_send()
            copy(0, dz, where, z, f, c, z, c * nf + f).wait_recv()
        else:
            for core, first in ((1, 0), (0, rows)):
                @pl.when(my_c == core)
                def _():
                    copy(first, dz, where, z, f, c, my_z, mine).wait_send()

                @pl.when(c == core)
                def _():
                    copy(first, dz, where, z, f, c, z, c * nf + f).wait_recv()

    own.wait()
    each_peer(finish)


def dot_nt(left, right):
    return lax.dot_general(left, right, (((1,), (1,)), ((), ())), preferred_element_type=jnp.float32)


def cross_kernel(
    nz, nf, rows, packed, scale,
    slots_ref, near_ref, code_ref, pair_ref, got_ref, table_ref, out_ref,
    where_ref, outer, rims, pairs, stage, sems,
):
    lanes = 2 * nf * rows
    half = rows // 2
    per_band = SEGLEN // 2 // (2 * nf)
    me = lax.axis_index("tiles")

    def place(slot):
        where_ref[slots_ref[slot]] = slot

    repeat(nz, place)

    def spread(slot):
        flat = got_ref[slot, :, rows : 2 * rows, :].reshape(lanes, EDGE)
        coded = dot_nt(table_ref[0 : 2 * EDGE, :], flat)
        outer[pl.ds(slot * 8, 8)] = coded.reshape(8, SIDE, lanes).astype(jnp.bfloat16)

    repeat(nz, spread)

    def entry(slot, edge):
        return where_ref[near_ref[slot, edge]] * 8 + code_ref[slot, edge]

    lane = lax.broadcasted_iota(jnp.int32, (1, EDGE), 1)

    def unpack(block):
        low = jnp.where(lane < PAIRS, block, jnp.zeros_like(block))
        if packed:
            return jnp.concatenate([low, jnp.where(lane < PAIRS, jnp.zeros_like(block), block)], axis=0)
        return low

    def sweep(slot):
        for edge in range(4):
            rims[slot, edge * SIDE : (edge + 1) * SIDE, :] = outer[entry(slot, edge)]
        own = jnp.concatenate([unpack(got_ref[slot, s, 2 * rows :, :]) for s in range(2 * nf)], axis=0)
        total = dot_nt(table_ref[256:384, :], own)
        total = total + jnp.dot(table_ref[384:512, :], rims[slot], preferred_element_type=jnp.float32)
        pairs[pl.ds(slot * 8, 8)] = total.reshape(8, SIDE // 2, lanes).astype(jnp.bfloat16)

    repeat(nz, sweep)

    def spectrum(slot):
        flat = got_ref[slot, :, 0:rows, :].reshape(lanes, COARSE)
        beyond = jnp.concatenate([pairs[entry(slot, edge)] for edge in range(4)], axis=0)
        total = dot_nt(table_ref[768:896, :], flat)
        total = total + jnp.dot(table_ref[512:640, :], rims[slot], preferred_element_type=jnp.float32)
        total = total + jnp.dot(table_ref[640:768, 0:PAIRS], beyond, preferred_element_type=jnp.float32)
        return total

    at = lax.broadcasted_iota(jnp.int32, (COARSE, lanes), 1)
    velocity = at >= lanes // 2
    height = spectrum(me).astype(jnp.bfloat16).astype(jnp.float32)
    height = jnp.where(velocity, pltpu.roll(height, lanes // 2, 1), 0.0)
    real_lane = at % rows < half
    turned = jnp.where(real_lane, pltpu.roll(height, lanes - half, 1), -pltpu.roll(height, half, 1))
    partner = []
    for k in range(2):
        total = spectrum(where_ref[pair_ref[0, k]])
        partner.append(jnp.where(velocity, total, 0.0).astype(jnp.bfloat16))
    partner = jnp.concatenate(partner, axis=0)
    both = jnp.concatenate([height, turned], axis=0).astype(jnp.bfloat16)
    at_both = lax.broadcasted_iota(jnp.int32, (2 * COARSE, lanes), 1) % per_band
    for f in range(per_band):
        chosen = jnp.where(at_both == f, both, jnp.zeros_like(both))
        cross = dot_nt(chosen, partner) * scale
        for k in range(2):
            for o in range(2):
                stage[f, k, o] = cross[o * COARSE : (o + 1) * COARSE, k * COARSE : (k + 1) * COARSE]
        pltpu.make_async_copy(stage.at[f], out_ref.at[0, :, :, f], sems.at[f]).start()
    for f in range(per_band):
        pltpu.make_async_copy(stage.at[f], out_ref.at[0, :, :, f], sems.at[f]).wait()


def shards(nz, nf, fields, slot_tile_ids, neighbour_tile_ids, neighbour_rotation_code, paired_tile_ids):
    samples = fields.shape[2]
    segments = samples // SEGLEN
    bands = 2 * nf
    per_band = SEGLEN // 2 // bands
    rows = 2 * segments * per_band
    lanes = bands * rows
    packed = rows % 32 == 0
    height = 2 * rows + (rows // 2 if packed else rows)
    sender, receiver = spatial_tables()
    times = time_table(segments, bands)
    scale = float(1.0 / (segments * nf * np.sum(hann() ** 2)))
    vmem = pl.BlockSpec(memory_space=pltpu.VMEM)
    smem = pl.BlockSpec(memory_space=pltpu.SMEM)
    anywhere = pl.BlockSpec(memory_space=pl.ANY)
    got = pl.pallas_call(
        functools.partial(exchange_kernel, nz, nf, rows, packed),
        out_shape=jax.ShapeDtypeStruct((nz, bands, height, EDGE), jnp.bfloat16),
        in_specs=[vmem, vmem, vmem],
        out_specs=anywhere,
        scratch_shapes=[
            pltpu.VMEM((bands, height, EDGE), jnp.bfloat16),
            pltpu.SemaphoreType.DMA((nz, bands)),
            pltpu.SemaphoreType.DMA((nz, bands)),
            pltpu.SemaphoreType.DMA,
        ],
        compiler_params=pltpu.CompilerParams(collective_id=0, has_side_effects=True),
        name="exchange",
    )(fields.reshape(samples, CELLS), jnp.asarray(sender), jnp.asarray(times))
    return pl.pallas_call(
        functools.partial(cross_kernel, nz, nf, rows, packed, scale),
        out_shape=jax.ShapeDtypeStruct((1, 2, 2, per_band, COARSE, COARSE), jnp.float32),
        in_specs=[smem, smem, smem, smem, vmem, vmem],
        out_specs=anywhere,
        scratch_shapes=[
            pltpu.SMEM((nz,), jnp.int32),
            pltpu.VMEM((nz * 8, SIDE, lanes), jnp.bfloat16),
            pltpu.VMEM((nz, EDGE, lanes), jnp.bfloat16),
            pltpu.VMEM((nz * 8, SIDE // 2, lanes), jnp.bfloat16),
            pltpu.VMEM((per_band, 2, 2, COARSE, COARSE), jnp.float32),
            pltpu.SemaphoreType.DMA((per_band,)),
        ],
        name="cross",
    )(slot_tile_ids, neighbour_tile_ids, neighbour_rotation_code, paired_tile_ids, got, jnp.asarray(receiver))


def solution(mesh):
    placed = (P("field", "tiles", ("groups", "freq"), None), P(), P(), P(), P("tiles", None))
    return jax.shard_map(
        functools.partial(shards, mesh.shape["tiles"], mesh.shape["freq"]),
        mesh=mesh,
        in_specs=placed,
        out_specs=P(("groups", "tiles"), None, None, ("freq", "field"), None, None),
        check_vma=False,
    )
```

```python
import functools

import jax
import jax.numpy as jnp
import numpy as np
from jax import lax
from jax.experimental import pallas as pl
from jax.experimental.pallas import tpu as pltpu
from jax.sharding import PartitionSpec as P

SIDE = 32
SEGLEN = 64
CELLS = SIDE * SIDE
EDGE = 4 * SIDE
PAIRS = EDGE // 2
COARSE = CELLS // 8
CHUNKS = 2
MESH = pl.DeviceIdType.MESH


def smooth_cells(field, rims):
    padded = np.zeros(field.shape[:-2] + (SIDE + 2, SIDE + 2))
    padded[..., 1:-1, 1:-1] = field
    padded[..., 0, 1:-1] = rims[..., 0, :]
    padded[..., 1:-1, -1] = rims[..., 1, :]
    padded[..., -1, 1:-1] = rims[..., 2, :]
    padded[..., 1:-1, 0] = rims[..., 3, :]
    around = padded[..., :-2, 1:-1] + padded[..., 2:, 1:-1] + padded[..., 1:-1, :-2] + padded[..., 1:-1, 2:]
    return 0.25 * around


def coarse_cells(field):
    blocks = field.reshape(field.shape[:-2] + (SIDE // 2, 2, SIDE // 4, 4))
    return blocks.sum(axis=(-3, -1)).reshape(field.shape[:-2] + (COARSE,))


def edges_of(field):
    return np.stack([field[..., 0, :], field[..., :, -1], field[..., -1, :], field[..., :, 0]], axis=-2)


def edge_pairs(field):
    edges = edges_of(field)
    return edges.reshape(edges.shape[:-2] + (PAIRS, 2)).sum(axis=-1)


def spatial_tables():
    cells = np.eye(CELLS).reshape(CELLS, SIDE, SIDE)
    rims = np.eye(EDGE).reshape(EDGE, 4, SIDE)
    cell_zero = np.zeros((EDGE, SIDE, SIDE))
    rim_zero = np.zeros((CELLS, 4, SIDE))
    once = smooth_cells(cells, rim_zero)
    rim_once = smooth_cells(cell_zero, rims)
    own_coarse = coarse_cells(smooth_cells(once, rim_zero))
    outer = edges_of(cells).reshape(CELLS, EDGE)
    own_pairs = edge_pairs(once)
    sender = np.concatenate([own_coarse, outer, own_pairs, own_pairs], axis=1)
    rim_coarse = coarse_cells(smooth_cells(rim_once, np.zeros((EDGE, 4, SIDE)))).T
    rim_pairs = edge_pairs(rim_once).T
    pair_rims = np.repeat(np.eye(PAIRS), 2, axis=1).reshape(PAIRS, 4, SIDE)
    pair_coarse = coarse_cells(smooth_cells(np.zeros((PAIRS, SIDE, SIDE)), pair_rims)).T * 0.5
    pair_coarse = pair_coarse * 1.0
    flip = np.kron(np.eye(4), np.eye(SIDE)[::-1])
    pair_flip = np.kron(np.eye(4), np.eye(SIDE // 2)[::-1])
    both = np.concatenate([np.eye(EDGE), flip])
    pair_both = np.concatenate([np.eye(PAIRS), pair_flip])
    pair_own = np.concatenate([pair_both, pair_both], axis=1)
    pair_rim = pair_both @ rim_pairs
    pair_coarse = np.concatenate([pair_coarse, np.zeros((COARSE, EDGE - PAIRS))], axis=1)
    receiver = np.concatenate([both, pair_own, pair_rim, rim_coarse, pair_coarse, np.eye(COARSE)])
    return sender.astype(jnp.bfloat16), receiver.astype(jnp.bfloat16)


def hann():
    return 0.5 - 0.5 * np.cos(2.0 * np.pi * np.arange(SEGLEN) / SEGLEN)


def time_table(segments, bands):
    per_band = SEGLEN // 2 // bands
    window = hann()
    table = np.zeros((bands, 2, segments, per_band, segments, SEGLEN))
    for band in range(bands):
        for inner in range(per_band):
            angles = 2.0 * np.pi * (((band * per_band + inner) * np.arange(SEGLEN)) % SEGLEN) / SEGLEN
            for segment in range(segments):
                table[band, 0, segment, inner, segment] = window * np.cos(angles)
                table[band, 1, segment, inner, segment] = -window * np.sin(angles)
    table = table.reshape(bands * 2 * segments * per_band, segments * SEGLEN).astype(np.float32)
    upper = table.astype(jnp.bfloat16)
    lower = (table - upper.astype(np.float32)).astype(jnp.bfloat16)
    return np.concatenate([upper, lower, upper], axis=1)


def repeat(count, body):
    if count <= 4:
        for step in range(count):
            body(step)
    else:
        lax.fori_loop(0, count, lambda step, carry: (body(step), carry)[1], 0)


def exchange_kernel(nz, nf, rows, packed, field_hbm, spatial_hbm, time_hbm, *refs):
    kept, (out_ref, *copies) = refs[:5], refs[5:11]
    field_ref, spatial_ref, time_ref, send, send_sem, recv_sem, load_sem, own_sem, keep_sem = refs[11:]
    group = lax.axis_index("groups")
    my_z = lax.axis_index("tiles")
    my_f = lax.axis_index("freq")
    my_c = lax.axis_index("field")
    last = send.shape[1]
    bands = 2 * nf

    def peers(dz, visit):
        z = lax.rem(my_z + dz, nz)
        for df in range(nf):
            for dc in range(2):
                yield_at = df * 2 + dc
                f = lax.rem(my_f + df, nf)
                c = lax.rem(my_c + dc, 2)
                visit(dz, yield_at, z, f, c)

    def each_peer(visit):
        def same(dz, where, z, f, c):
            if where:
                visit(True, dz, where, z, f, c)

        peers(0, same)
        repeat(nz - 1, lambda step: peers(step + 1, functools.partial(visit, False)))

    barrier = pltpu.get_barrier_semaphore()

    def greet(near, dz, where, z, f, c):
        pl.semaphore_signal(barrier, inc=1, device_id=(group, z, f, c), device_id_type=MESH)

    each_peer(greet)

    loads = []
    for chunk in range(CHUNKS):
        cells = pl.ds(chunk * CELLS // CHUNKS, CELLS // CHUNKS)
        loads.append((
            pltpu.make_async_copy(field_hbm.at[:, cells], field_ref.at[:, cells], load_sem.at[2 * chunk]),
            pltpu.make_async_copy(spatial_hbm.at[cells, :], spatial_ref.at[cells, :], load_sem.at[2 * chunk + 1]),
        ))
    loads.append((pltpu.make_async_copy(time_hbm, time_ref, load_sem.at[2 * CHUNKS]),))
    for load in loads:
        for part in load:
            part.start()
    keeps = [pltpu.make_async_copy(a, b, keep_sem.at[i]) for i, (a, b) in enumerate(zip(kept, copies))]
    for keep in keeps:
        keep.start()
    mapped = None
    for chunk in range(CHUNKS):
        for part in loads[chunk]:
            part.wait()
        cells = pl.ds(chunk * CELLS // CHUNKS, CELLS // CHUNKS)
        term = jnp.dot(field_ref[:, cells], spatial_ref[cells, :], preferred_element_type=jnp.float32)
        mapped = term if mapped is None else mapped + term
    loads[CHUNKS][0].wait()
    upper = mapped.astype(jnp.bfloat16)
    lower = (mapped - upper.astype(jnp.float32)).astype(jnp.bfloat16)
    spectra = jnp.dot(
        time_ref[...], jnp.concatenate([upper, upper, lower], axis=0), preferred_element_type=jnp.float32
    )
    half = rows // 2
    lane = lax.broadcasted_iota(jnp.int32, (half, EDGE), 1)
    for band in range(bands):
        block = spectra[band * rows : (band + 1) * rows]
        send[band, 0:rows, :] = block[:, 0:COARSE].astype(jnp.bfloat16)
        send[band, rows : 2 * rows, :] = block[:, COARSE : COARSE + EDGE].astype(jnp.bfloat16)
        pairs = block[:, COARSE + EDGE :]
        if packed:
            pairs = jnp.where(lane < PAIRS, pairs[:half], pairs[half:])
        send[band, 2 * rows :, :] = pairs.astype(jnp.bfloat16)

    pl.semaphore_wait(barrier, nz * nf * 2 - 1)

    mine = my_c * nf + my_f

    def copy(first, dz, where, z, f, c, source_z, source):
        return pltpu.make_async_remote_copy(
            src_ref=send.at[f * 2 + c, pl.ds(first, last - first), :],
            dst_ref=out_ref.at[source_z, source, pl.ds(first, last - first), :],
            send_sem=send_sem.at[dz, where],
            recv_sem=recv_sem.at[source_z, source],
            device_id=(group, z, f, c),
            device_id_type=MESH,
        )

    def start(near, dz, where, z, f, c):
        if near:
            copy(0, dz, where, z, f, c, my_z, mine).start()
        else:
            @pl.when(my_c == 1)
            def _():
                copy(0, dz, where, z, f, c, my_z, mine).start()

            @pl.when(my_c == 0)
            def _():
                copy(rows, dz, where, z, f, c, my_z, mine).start()

    each_peer(start)
    own = pltpu.make_async_copy(send.at[my_f * 2 + my_c], out_ref.at[my_z, mine], own_sem)
    own.start()

    def finish(near, dz, where, z, f, c):
        if near:
            copy(0, dz, where, z, f, c, my_z, mine).wait_send()
            copy(0, dz, where, z, f, c, z, c * nf + f).wait_recv()
        else:
            for core, first in ((1, 0), (0, rows)):
                @pl.when(my_c == core)
                def _():
                    copy(first, dz, where, z, f, c, my_z, mine).wait_send()

                @pl.when(c == core)
                def _():
                    copy(first, dz, where, z, f, c, z, c * nf + f).wait_recv()

    own.wait()
    for keep in keeps:
        keep.wait()
    each_peer(finish)


def dot_nt(left, right):
    return lax.dot_general(left, right, (((1,), (1,)), ((), ())), preferred_element_type=jnp.float32)


def cross_kernel(
    nz, nf, rows, packed, scale,
    slots_ref, near_ref, code_ref, pair_ref, got_ref, table_ref, out_ref,
    where_ref, outer, rims, pairs, stage, sems,
):
    lanes = 2 * nf * rows
    half = rows // 2
    per_band = SEGLEN // 2 // (2 * nf)
    me = lax.axis_index("tiles")

    def place(slot):
        where_ref[slots_ref[slot]] = slot

    repeat(nz, place)

    def spread(slot):
        flat = got_ref[slot, :, rows : 2 * rows, :].reshape(lanes, EDGE)
        coded = dot_nt(table_ref[0 : 2 * EDGE, :], flat)
        outer[pl.ds(slot * 8, 8)] = coded.reshape(8, SIDE, lanes).astype(jnp.bfloat16)

    repeat(nz, spread)

    def entry(slot, edge):
        return where_ref[near_ref[slot, edge]] * 8 + code_ref[slot, edge]

    lane = lax.broadcasted_iota(jnp.int32, (1, EDGE), 1)

    def unpack(block):
        low = jnp.where(lane < PAIRS, block, jnp.zeros_like(block))
        if packed:
            return jnp.concatenate([low, jnp.where(lane < PAIRS, jnp.zeros_like(block), block)], axis=0)
        return low

    def sweep(slot):
        for edge in range(4):
            rims[slot, edge * SIDE : (edge + 1) * SIDE, :] = outer[entry(slot, edge)]
        own = jnp.concatenate([unpack(got_ref[slot, s, 2 * rows :, :]) for s in range(2 * nf)], axis=0)
        total = dot_nt(table_ref[256:384, :], own)
        total = total + jnp.dot(table_ref[384:512, :], rims[slot], preferred_element_type=jnp.float32)
        pairs[pl.ds(slot * 8, 8)] = total.reshape(8, SIDE // 2, lanes).astype(jnp.bfloat16)

    repeat(nz, sweep)

    def spectrum(slot):
        flat = got_ref[slot, :, 0:rows, :].reshape(lanes, COARSE)
        beyond = jnp.concatenate([pairs[entry(slot, edge)] for edge in range(4)], axis=0)
        total = dot_nt(table_ref[768:896, :], flat)
        total = total + jnp.dot(table_ref[512:640, :], rims[slot], preferred_element_type=jnp.float32)
        total = total + jnp.dot(table_ref[640:768, 0:PAIRS], beyond, preferred_element_type=jnp.float32)
        return total

    at = lax.broadcasted_iota(jnp.int32, (COARSE, lanes), 1)
    velocity = at >= lanes // 2
    height = spectrum(me).astype(jnp.bfloat16).astype(jnp.float32)
    height = jnp.where(velocity, pltpu.roll(height, lanes // 2, 1), 0.0)
    real_lane = at % rows < half
    turned = jnp.where(real_lane, pltpu.roll(height, lanes - half, 1), -pltpu.roll(height, half, 1))
    partner = []
    for k in range(2):
        total = spectrum(where_ref[pair_ref[0, k]])
        partner.append(jnp.where(velocity, total, 0.0).astype(jnp.bfloat16))
    partner = jnp.concatenate(partner, axis=0)
    both = jnp.concatenate([height, turned], axis=0).astype(jnp.bfloat16)
    at_both = lax.broadcasted_iota(jnp.int32, (2 * COARSE, lanes), 1) % per_band
    for f in range(per_band):
        chosen = jnp.where(at_both == f, both, jnp.zeros_like(both))
        cross = dot_nt(chosen, partner) * scale
        for k in range(2):
            for o in range(2):
                stage[f, k, o] = cross[o * COARSE : (o + 1) * COARSE, k * COARSE : (k + 1) * COARSE]
        pltpu.make_async_copy(stage.at[f], out_ref.at[0, :, :, f], sems.at[f]).start()
    for f in range(per_band):
        pltpu.make_async_copy(stage.at[f], out_ref.at[0, :, :, f], sems.at[f]).wait()


def shards(nz, nf, fields, slot_tile_ids, neighbour_tile_ids, neighbour_rotation_code, paired_tile_ids):
    samples = fields.shape[2]
    segments = samples // SEGLEN
    bands = 2 * nf
    per_band = SEGLEN // 2 // bands
    rows = 2 * segments * per_band
    lanes = bands * rows
    packed = rows % 32 == 0
    height = 2 * rows + (rows // 2 if packed else rows)
    sender, receiver = spatial_tables()
    times = time_table(segments, bands)
    scale = float(1.0 / (segments * nf * np.sum(hann() ** 2)))
    vmem = pl.BlockSpec(memory_space=pltpu.VMEM)
    smem = pl.BlockSpec(memory_space=pltpu.SMEM)
    hbm = pl.BlockSpec(memory_space=pltpu.HBM)
    anywhere = pl.BlockSpec(memory_space=pl.ANY)
    ids = (slot_tile_ids, neighbour_tile_ids, neighbour_rotation_code, paired_tile_ids)
    kept = ids + (jnp.asarray(receiver),)
    got, *kept = pl.pallas_call(
        functools.partial(exchange_kernel, nz, nf, rows, packed),
        out_shape=[jax.ShapeDtypeStruct((nz, bands, height, EDGE), jnp.bfloat16)]
        + [jax.ShapeDtypeStruct(a.shape, a.dtype) for a in kept],
        in_specs=[hbm] * 8,
        out_specs=[anywhere] * 6,
        scratch_shapes=[
            pltpu.VMEM((samples, CELLS), jnp.bfloat16),
            pltpu.VMEM(sender.shape, jnp.bfloat16),
            pltpu.VMEM(times.shape, jnp.bfloat16),
            pltpu.VMEM((bands, height, EDGE), jnp.bfloat16),
            pltpu.SemaphoreType.DMA((nz, bands)),
            pltpu.SemaphoreType.DMA((nz, bands)),
            pltpu.SemaphoreType.DMA((2 * CHUNKS + 1,)),
            pltpu.SemaphoreType.DMA,
            pltpu.SemaphoreType.DMA((5,)),
        ],
        compiler_params=pltpu.CompilerParams(
            collective_id=0, has_side_effects=True, vmem_limit_bytes=4 << 20
        ),
        name="exchange",
    )(*[pltpu.with_memory_space_constraint(a, pltpu.HBM) for a in
         (fields.reshape(samples, CELLS), jnp.asarray(sender), jnp.asarray(times), *kept)])
    return pl.pallas_call(
        functools.partial(cross_kernel, nz, nf, rows, packed, scale),
        out_shape=jax.ShapeDtypeStruct((1, 2, 2, per_band, COARSE, COARSE), jnp.float32),
        in_specs=[smem, smem, smem, smem, vmem, vmem],
        out_specs=anywhere,
        scratch_shapes=[
            pltpu.SMEM((nz,), jnp.int32),
            pltpu.VMEM((nz * 8, SIDE, lanes), jnp.bfloat16),
            pltpu.VMEM((nz, EDGE, lanes), jnp.bfloat16),
            pltpu.VMEM((nz * 8, SIDE // 2, lanes), jnp.bfloat16),
            pltpu.VMEM((per_band, 2, 2, COARSE, COARSE), jnp.float32),
            pltpu.SemaphoreType.DMA((per_band,)),
        ],
        compiler_params=pltpu.CompilerParams(vmem_limit_bytes=max(8, nz) << 20),
        name="cross",
    )(*kept[:4], got, kept[4])


def solution(mesh):
    placed = (P("field", "tiles", ("groups", "freq"), None), P(), P(), P(), P("tiles", None))
    return jax.shard_map(
        functools.partial(shards, mesh.shape["tiles"], mesh.shape["freq"]),
        mesh=mesh,
        in_specs=placed,
        out_specs=P(("groups", "tiles"), None, None, ("freq", "field"), None, None),
        check_vma=False,
    )
```

```python
import functools

import jax
import jax.numpy as jnp
import numpy as np
from jax import lax
from jax.experimental import pallas as pl
from jax.experimental.pallas import tpu as pltpu
from jax.sharding import PartitionSpec as P

SIDE = 32
SEGLEN = 64
CELLS = SIDE * SIDE
EDGE = 4 * SIDE
PAIRS = EDGE // 2
COARSE = CELLS // 8
CHUNKS = 2
MESH = pl.DeviceIdType.MESH


def smooth_cells(field, rims):
    padded = np.zeros(field.shape[:-2] + (SIDE + 2, SIDE + 2))
    padded[..., 1:-1, 1:-1] = field
    padded[..., 0, 1:-1] = rims[..., 0, :]
    padded[..., 1:-1, -1] = rims[..., 1, :]
    padded[..., -1, 1:-1] = rims[..., 2, :]
    padded[..., 1:-1, 0] = rims[..., 3, :]
    around = padded[..., :-2, 1:-1] + padded[..., 2:, 1:-1] + padded[..., 1:-1, :-2] + padded[..., 1:-1, 2:]
    return 0.25 * around


def coarse_cells(field):
    blocks = field.reshape(field.shape[:-2] + (SIDE // 2, 2, SIDE // 4, 4))
    return blocks.sum(axis=(-3, -1)).reshape(field.shape[:-2] + (COARSE,))


def edges_of(field):
    return np.stack([field[..., 0, :], field[..., :, -1], field[..., -1, :], field[..., :, 0]], axis=-2)


def edge_pairs(field):
    edges = edges_of(field)
    return edges.reshape(edges.shape[:-2] + (PAIRS, 2)).sum(axis=-1)


def spatial_tables():
    cells = np.eye(CELLS).reshape(CELLS, SIDE, SIDE)
    rims = np.eye(EDGE).reshape(EDGE, 4, SIDE)
    cell_zero = np.zeros((EDGE, SIDE, SIDE))
    rim_zero = np.zeros((CELLS, 4, SIDE))
    once = smooth_cells(cells, rim_zero)
    rim_once = smooth_cells(cell_zero, rims)
    own_coarse = coarse_cells(smooth_cells(once, rim_zero))
    outer = edges_of(cells).reshape(CELLS, EDGE)
    own_pairs = edge_pairs(once)
    sender = np.concatenate([own_coarse, outer, own_pairs, own_pairs], axis=1)
    rim_coarse = coarse_cells(smooth_cells(rim_once, np.zeros((EDGE, 4, SIDE)))).T
    rim_pairs = edge_pairs(rim_once).T
    pair_rims = np.repeat(np.eye(PAIRS), 2, axis=1).reshape(PAIRS, 4, SIDE)
    pair_coarse = coarse_cells(smooth_cells(np.zeros((PAIRS, SIDE, SIDE)), pair_rims)).T * 0.5
    pair_coarse = pair_coarse * 1.0
    flip = np.kron(np.eye(4), np.eye(SIDE)[::-1])
    pair_flip = np.kron(np.eye(4), np.eye(SIDE // 2)[::-1])
    both = np.concatenate([np.eye(EDGE), flip])
    pair_both = np.concatenate([np.eye(PAIRS), pair_flip])
    pair_own = np.concatenate([pair_both, pair_both], axis=1)
    pair_rim = pair_both @ rim_pairs
    pair_coarse = np.concatenate([pair_coarse, np.zeros((COARSE, EDGE - PAIRS))], axis=1)
    receiver = np.concatenate([both, pair_own, pair_rim, rim_coarse, pair_coarse, np.eye(COARSE)])
    return sender.astype(jnp.bfloat16), receiver.astype(jnp.bfloat16)


def hann():
    return 0.5 - 0.5 * np.cos(2.0 * np.pi * np.arange(SEGLEN) / SEGLEN)


def time_table(segments, bands):
    per_band = SEGLEN // 2 // bands
    window = hann()
    table = np.zeros((bands, 2, segments, per_band, segments, SEGLEN))
    for band in range(bands):
        for inner in range(per_band):
            angles = 2.0 * np.pi * (((band * per_band + inner) * np.arange(SEGLEN)) % SEGLEN) / SEGLEN
            for segment in range(segments):
                table[band, 0, segment, inner, segment] = window * np.cos(angles)
                table[band, 1, segment, inner, segment] = -window * np.sin(angles)
    table = table.reshape(bands * 2 * segments * per_band, segments * SEGLEN).astype(np.float32)
    upper = table.astype(jnp.bfloat16)
    lower = (table - upper.astype(np.float32)).astype(jnp.bfloat16)
    return np.concatenate([upper, lower, upper], axis=1)


def repeat(count, body):
    if count <= 4:
        for step in range(count):
            body(step)
    else:
        lax.fori_loop(0, count, lambda step, carry: (body(step), carry)[1], 0)


def exchange_kernel(nz, nf, rows, packed, field_hbm, spatial_hbm, time_hbm, *refs):
    kept, (out_ref, *copies) = refs[:5], refs[5:11]
    field_ref, spatial_ref, time_ref, send, send_sem, recv_sem, load_sem, own_sem, keep_sem = refs[11:]
    group = lax.axis_index("groups")
    my_z = lax.axis_index("tiles")
    my_f = lax.axis_index("freq")
    my_c = lax.axis_index("field")
    last = send.shape[1]
    bands = 2 * nf

    def peers(dz, visit):
        z = lax.rem(my_z + dz, nz)
        for df in range(nf):
            for dc in range(2):
                yield_at = df * 2 + dc
                f = lax.rem(my_f + df, nf)
                c = lax.rem(my_c + dc, 2)
                visit(dz, yield_at, z, f, c)

    def each_peer(visit):
        def same(dz, where, z, f, c):
            if where:
                visit(True, dz, where, z, f, c)

        repeat(nz - 1, lambda step: peers(step + 1, functools.partial(visit, False)))
        peers(0, same)

    barrier = pltpu.get_barrier_semaphore()

    def greet(near, dz, where, z, f, c):
        pl.semaphore_signal(barrier, inc=1, device_id=(group, z, f, c), device_id_type=MESH)


    loads = []
    for chunk in range(CHUNKS):
        cells = pl.ds(chunk * CELLS // CHUNKS, CELLS // CHUNKS)
        loads.append((
            pltpu.make_async_copy(field_hbm.at[:, cells], field_ref.at[:, cells], load_sem.at[2 * chunk]),
            pltpu.make_async_copy(spatial_hbm.at[cells, :], spatial_ref.at[cells, :], load_sem.at[2 * chunk + 1]),
        ))
    loads.append((pltpu.make_async_copy(time_hbm, time_ref, load_sem.at[2 * CHUNKS]),))
    for load in loads:
        for part in load:
            part.start()
    each_peer(greet)
    keeps = [pltpu.make_async_copy(a, b, keep_sem.at[i]) for i, (a, b) in enumerate(zip(kept, copies))]
    mapped = None
    for chunk in range(CHUNKS):
        for part in loads[chunk]:
            part.wait()
        cells = pl.ds(chunk * CELLS // CHUNKS, CELLS // CHUNKS)
        term = jnp.dot(field_ref[:, cells], spatial_ref[cells, :], preferred_element_type=jnp.float32)
        mapped = term if mapped is None else mapped + term
    loads[CHUNKS][0].wait()
    for keep in keeps:
        keep.start()
    upper = mapped.astype(jnp.bfloat16)
    lower = (mapped - upper.astype(jnp.float32)).astype(jnp.bfloat16)
    spectra = jnp.dot(
        time_ref[...], jnp.concatenate([upper, upper, lower], axis=0), preferred_element_type=jnp.float32
    )
    half = rows // 2
    lane = lax.broadcasted_iota(jnp.int32, (half, EDGE), 1)
    for band in range(bands):
        block = spectra[band * rows : (band + 1) * rows]
        send[band, 0:rows, :] = block[:, 0:COARSE].astype(jnp.bfloat16)
        send[band, rows : 2 * rows, :] = block[:, COARSE : COARSE + EDGE].astype(jnp.bfloat16)
        pairs = block[:, COARSE + EDGE :]
        if packed:
            pairs = jnp.where(lane < PAIRS, pairs[:half], pairs[half:])
        send[band, 2 * rows :, :] = pairs.astype(jnp.bfloat16)

    pl.semaphore_wait(barrier, nz * nf * 2 - 1)

    mine = my_c * nf + my_f

    def copy(first, dz, where, z, f, c, source_z, source):
        return pltpu.make_async_remote_copy(
            src_ref=send.at[f * 2 + c, pl.ds(first, last - first), :],
            dst_ref=out_ref.at[source_z, source, pl.ds(first, last - first), :],
            send_sem=send_sem.at[dz, where],
            recv_sem=recv_sem.at[source_z, source],
            device_id=(group, z, f, c),
            device_id_type=MESH,
        )

    def start(near, dz, where, z, f, c):
        if near:
            copy(0, dz, where, z, f, c, my_z, mine).start()
        else:
            @pl.when(my_c == 1)
            def _():
                copy(0, dz, where, z, f, c, my_z, mine).start()

            @pl.when(my_c == 0)
            def _():
                copy(rows, dz, where, z, f, c, my_z, mine).start()

    each_peer(start)
    own = pltpu.make_async_copy(send.at[my_f * 2 + my_c], out_ref.at[my_z, mine], own_sem)
    own.start()

    def finish(near, dz, where, z, f, c):
        if near:
            copy(0, dz, where, z, f, c, my_z, mine).wait_send()
            copy(0, dz, where, z, f, c, z, c * nf + f).wait_recv()
        else:
            for core, first in ((1, 0), (0, rows)):
                @pl.when(my_c == core)
                def _():
                    copy(first, dz, where, z, f, c, my_z, mine).wait_send()

                @pl.when(c == core)
                def _():
                    copy(first, dz, where, z, f, c, z, c * nf + f).wait_recv()

    own.wait()
    for keep in keeps:
        keep.wait()
    each_peer(finish)


def dot_nt(left, right):
    return lax.dot_general(left, right, (((1,), (1,)), ((), ())), preferred_element_type=jnp.float32)


def cross_kernel(
    nz, nf, rows, packed, scale,
    slots_ref, near_ref, code_ref, pair_ref, got_ref, table_ref, out_ref,
    where_ref, outer, rims, pairs, stage, sems,
):
    lanes = 2 * nf * rows
    half = rows // 2
    per_band = SEGLEN // 2 // (2 * nf)
    me = lax.axis_index("tiles")

    def place(slot):
        where_ref[slots_ref[slot]] = slot

    repeat(nz, place)

    def spread(slot):
        flat = got_ref[slot, :, rows : 2 * rows, :].reshape(lanes, EDGE)
        coded = dot_nt(table_ref[0 : 2 * EDGE, :], flat)
        outer[pl.ds(slot * 8, 8)] = coded.reshape(8, SIDE, lanes).astype(jnp.bfloat16)

    repeat(nz, spread)

    def entry(slot, edge):
        return where_ref[near_ref[slot, edge]] * 8 + code_ref[slot, edge]

    lane = lax.broadcasted_iota(jnp.int32, (1, EDGE), 1)

    def unpack(block):
        low = jnp.where(lane < PAIRS, block, jnp.zeros_like(block))
        if packed:
            return jnp.concatenate([low, jnp.where(lane < PAIRS, jnp.zeros_like(block), block)], axis=0)
        return low

    def sweep(slot):
        for edge in range(4):
            rims[slot, edge * SIDE : (edge + 1) * SIDE, :] = outer[entry(slot, edge)]
        own = jnp.concatenate([unpack(got_ref[slot, s, 2 * rows :, :]) for s in range(2 * nf)], axis=0)
        total = dot_nt(table_ref[256:384, :], own)
        total = total + jnp.dot(table_ref[384:512, :], rims[slot], preferred_element_type=jnp.float32)
        pairs[pl.ds(slot * 8, 8)] = total.reshape(8, SIDE // 2, lanes).astype(jnp.bfloat16)

    repeat(nz, sweep)

    def spectrum(slot):
        flat = got_ref[slot, :, 0:rows, :].reshape(lanes, COARSE)
        beyond = jnp.concatenate([pairs[entry(slot, edge)] for edge in range(4)], axis=0)
        total = dot_nt(table_ref[768:896, :], flat)
        total = total + jnp.dot(table_ref[512:640, :], rims[slot], preferred_element_type=jnp.float32)
        total = total + jnp.dot(table_ref[640:768, 0:PAIRS], beyond, preferred_element_type=jnp.float32)
        return total

    at = lax.broadcasted_iota(jnp.int32, (COARSE, lanes), 1)
    velocity = at >= lanes // 2
    height = spectrum(me).astype(jnp.bfloat16).astype(jnp.float32)
    height = jnp.where(velocity, pltpu.roll(height, lanes // 2, 1), 0.0)
    real_lane = at % rows < half
    turned = jnp.where(real_lane, pltpu.roll(height, lanes - half, 1), -pltpu.roll(height, half, 1))
    partner = []
    for k in range(2):
        total = spectrum(where_ref[pair_ref[0, k]])
        partner.append(jnp.where(velocity, total, 0.0).astype(jnp.bfloat16))
    partner = jnp.concatenate(partner, axis=0)
    both = jnp.concatenate([height, turned], axis=0).astype(jnp.bfloat16)
    at_both = lax.broadcasted_iota(jnp.int32, (2 * COARSE, lanes), 1) % per_band
    for f in range(per_band):
        chosen = jnp.where(at_both == f, both, jnp.zeros_like(both))
        cross = dot_nt(chosen, partner) * scale
        for k in range(2):
            for o in range(2):
                stage[f, k, o] = cross[o * COARSE : (o + 1) * COARSE, k * COARSE : (k + 1) * COARSE]
        pltpu.make_async_copy(stage.at[f], out_ref.at[0, :, :, f], sems.at[f]).start()
    for f in range(per_band):
        pltpu.make_async_copy(stage.at[f], out_ref.at[0, :, :, f], sems.at[f]).wait()


def shards(nz, nf, fields, slot_tile_ids, neighbour_tile_ids, neighbour_rotation_code, paired_tile_ids):
    samples = fields.shape[2]
    segments = samples // SEGLEN
    bands = 2 * nf
    per_band = SEGLEN // 2 // bands
    rows = 2 * segments * per_band
    lanes = bands * rows
    packed = rows % 32 == 0
    height = 2 * rows + (rows // 2 if packed else rows)
    sender, receiver = spatial_tables()
    times = time_table(segments, bands)
    scale = float(1.0 / (segments * nf * np.sum(hann() ** 2)))
    vmem = pl.BlockSpec(memory_space=pltpu.VMEM)
    smem = pl.BlockSpec(memory_space=pltpu.SMEM)
    hbm = pl.BlockSpec(memory_space=pltpu.HBM)
    anywhere = pl.BlockSpec(memory_space=pl.ANY)
    ids = (slot_tile_ids, neighbour_tile_ids, neighbour_rotation_code, paired_tile_ids)
    kept = ids + (jnp.asarray(receiver),)
    got, *kept = pl.pallas_call(
        functools.partial(exchange_kernel, nz, nf, rows, packed),
        out_shape=[jax.ShapeDtypeStruct((nz, bands, height, EDGE), jnp.bfloat16)]
        + [jax.ShapeDtypeStruct(a.shape, a.dtype) for a in kept],
        in_specs=[hbm] * 8,
        out_specs=[anywhere] * 6,
        scratch_shapes=[
            pltpu.VMEM((samples, CELLS), jnp.bfloat16),
            pltpu.VMEM(sender.shape, jnp.bfloat16),
            pltpu.VMEM(times.shape, jnp.bfloat16),
            pltpu.VMEM((bands, height, EDGE), jnp.bfloat16),
            pltpu.SemaphoreType.DMA((nz, bands)),
            pltpu.SemaphoreType.DMA((nz, bands)),
            pltpu.SemaphoreType.DMA((2 * CHUNKS + 1,)),
            pltpu.SemaphoreType.DMA,
            pltpu.SemaphoreType.DMA((5,)),
        ],
        compiler_params=pltpu.CompilerParams(
            collective_id=0, has_side_effects=True, vmem_limit_bytes=4 << 20
        ),
        name="exchange",
    )(*[pltpu.with_memory_space_constraint(a, pltpu.HBM) for a in
         (fields.reshape(samples, CELLS), jnp.asarray(sender), jnp.asarray(times), *kept)])
    return pl.pallas_call(
        functools.partial(cross_kernel, nz, nf, rows, packed, scale),
        out_shape=jax.ShapeDtypeStruct((1, 2, 2, per_band, COARSE, COARSE), jnp.float32),
        in_specs=[smem, smem, smem, smem, vmem, vmem],
        out_specs=anywhere,
        scratch_shapes=[
            pltpu.SMEM((nz,), jnp.int32),
            pltpu.VMEM((nz * 8, SIDE, lanes), jnp.bfloat16),
            pltpu.VMEM((nz, EDGE, lanes), jnp.bfloat16),
            pltpu.VMEM((nz * 8, SIDE // 2, lanes), jnp.bfloat16),
            pltpu.VMEM((per_band, 2, 2, COARSE, COARSE), jnp.float32),
            pltpu.SemaphoreType.DMA((per_band,)),
        ],
        compiler_params=pltpu.CompilerParams(vmem_limit_bytes=max(8, nz) << 20),
        name="cross",
    )(*kept[:4], got, kept[4])


def solution(mesh):
    placed = (P("field", "tiles", ("groups", "freq"), None), P(), P(), P(), P("tiles", None))
    return jax.shard_map(
        functools.partial(shards, mesh.shape["tiles"], mesh.shape["freq"]),
        mesh=mesh,
        in_specs=placed,
        out_specs=P(("groups", "tiles"), None, None, ("freq", "field"), None, None),
        check_vma=False,
    )
```

```python
import functools

import jax
import jax.numpy as jnp
import numpy as np
from jax import lax
from jax.experimental import pallas as pl
from jax.experimental.pallas import tpu as pltpu
from jax.sharding import PartitionSpec as P

SIDE = 32
SEGLEN = 64
CELLS = SIDE * SIDE
EDGE = 4 * SIDE
PAIRS = EDGE // 2
COARSE = CELLS // 8
CHUNKS = 2
MESH = pl.DeviceIdType.MESH


def smooth_cells(field, rims):
    padded = np.zeros(field.shape[:-2] + (SIDE + 2, SIDE + 2))
    padded[..., 1:-1, 1:-1] = field
    padded[..., 0, 1:-1] = rims[..., 0, :]
    padded[..., 1:-1, -1] = rims[..., 1, :]
    padded[..., -1, 1:-1] = rims[..., 2, :]
    padded[..., 1:-1, 0] = rims[..., 3, :]
    around = padded[..., :-2, 1:-1] + padded[..., 2:, 1:-1] + padded[..., 1:-1, :-2] + padded[..., 1:-1, 2:]
    return 0.25 * around


def coarse_cells(field):
    blocks = field.reshape(field.shape[:-2] + (SIDE // 2, 2, SIDE // 4, 4))
    return blocks.sum(axis=(-3, -1)).reshape(field.shape[:-2] + (COARSE,))


def edges_of(field):
    return np.stack([field[..., 0, :], field[..., :, -1], field[..., -1, :], field[..., :, 0]], axis=-2)


def edge_pairs(field):
    edges = edges_of(field)
    return edges.reshape(edges.shape[:-2] + (PAIRS, 2)).sum(axis=-1)


def spatial_tables():
    cells = np.eye(CELLS).reshape(CELLS, SIDE, SIDE)
    rims = np.eye(EDGE).reshape(EDGE, 4, SIDE)
    cell_zero = np.zeros((EDGE, SIDE, SIDE))
    rim_zero = np.zeros((CELLS, 4, SIDE))
    once = smooth_cells(cells, rim_zero)
    rim_once = smooth_cells(cell_zero, rims)
    own_coarse = coarse_cells(smooth_cells(once, rim_zero))
    outer = edges_of(cells).reshape(CELLS, EDGE)
    own_pairs = edge_pairs(once)
    sender = np.concatenate([own_coarse, outer, own_pairs, own_pairs], axis=1)
    rim_coarse = coarse_cells(smooth_cells(rim_once, np.zeros((EDGE, 4, SIDE)))).T
    rim_pairs = edge_pairs(rim_once).T
    pair_rims = np.repeat(np.eye(PAIRS), 2, axis=1).reshape(PAIRS, 4, SIDE)
    pair_coarse = coarse_cells(smooth_cells(np.zeros((PAIRS, SIDE, SIDE)), pair_rims)).T * 0.5
    pair_coarse = pair_coarse * 1.0
    flip = np.kron(np.eye(4), np.eye(SIDE)[::-1])
    pair_flip = np.kron(np.eye(4), np.eye(SIDE // 2)[::-1])
    both = np.concatenate([np.eye(EDGE), flip])
    pair_both = np.concatenate([np.eye(PAIRS), pair_flip])
    pair_own = np.concatenate([pair_both, pair_both], axis=1)
    pair_rim = pair_both @ rim_pairs
    pair_coarse = np.concatenate([pair_coarse, np.zeros((COARSE, EDGE - PAIRS))], axis=1)
    receiver = np.concatenate([both, pair_own, pair_rim, rim_coarse, pair_coarse, np.eye(COARSE)])
    return sender.astype(jnp.bfloat16), receiver.astype(jnp.bfloat16)


def hann():
    return 0.5 - 0.5 * np.cos(2.0 * np.pi * np.arange(SEGLEN) / SEGLEN)


def time_table(segments, bands):
    per_band = SEGLEN // 2 // bands
    window = hann()
    table = np.zeros((bands, 2, segments, per_band, segments, SEGLEN))
    for band in range(bands):
        for inner in range(per_band):
            angles = 2.0 * np.pi * (((band * per_band + inner) * np.arange(SEGLEN)) % SEGLEN) / SEGLEN
            for segment in range(segments):
                table[band, 0, segment, inner, segment] = window * np.cos(angles)
                table[band, 1, segment, inner, segment] = -window * np.sin(angles)
    table = table.reshape(bands * 2 * segments * per_band, segments * SEGLEN).astype(np.float32)
    upper = table.astype(jnp.bfloat16)
    lower = (table - upper.astype(np.float32)).astype(jnp.bfloat16)
    return np.concatenate([upper, lower, upper], axis=1)


def repeat(count, body):
    if count <= 4:
        for step in range(count):
            body(step)
    else:
        lax.fori_loop(0, count, lambda step, carry: (body(step), carry)[1], 0)


def exchange_kernel(nz, nf, rows, packed, field_hbm, spatial_hbm, time_hbm, *refs):
    kept, (out_ref, *copies) = refs[:5], refs[5:11]
    field_ref, spatial_ref, time_ref, send, send_sem, recv_sem, load_sem, own_sem, keep_sem = refs[11:]
    group = lax.axis_index("groups")
    my_z = lax.axis_index("tiles")
    my_f = lax.axis_index("freq")
    my_c = lax.axis_index("field")
    last = send.shape[1]
    bands = 2 * nf

    def peers(dz, visit):
        z = lax.rem(my_z + dz, nz)
        for df in range(nf):
            for dc in range(2):
                yield_at = df * 2 + dc
                f = lax.rem(my_f + df, nf)
                c = lax.rem(my_c + dc, 2)
                visit(dz, yield_at, z, f, c)

    def each_peer(visit):
        def same(dz, where, z, f, c):
            if where:
                visit(True, dz, where, z, f, c)

        repeat(nz - 1, lambda step: peers(step + 1, functools.partial(visit, False)))
        peers(0, same)

    barrier = pltpu.get_barrier_semaphore()

    def greet(near, dz, where, z, f, c):
        pl.semaphore_signal(barrier, inc=1, device_id=(group, z, f, c), device_id_type=MESH)


    loads = []
    for chunk in range(CHUNKS):
        cells = pl.ds(chunk * CELLS // CHUNKS, CELLS // CHUNKS)
        loads.append((
            pltpu.make_async_copy(field_hbm.at[:, cells], field_ref.at[:, cells], load_sem.at[2 * chunk]),
            pltpu.make_async_copy(spatial_hbm.at[cells, :], spatial_ref.at[cells, :], load_sem.at[2 * chunk + 1]),
        ))
    loads.append((pltpu.make_async_copy(time_hbm, time_ref, load_sem.at[2 * CHUNKS]),))
    for load in loads:
        for part in load:
            part.start()
    each_peer(greet)
    keeps = [pltpu.make_async_copy(a, b, keep_sem.at[i]) for i, (a, b) in enumerate(zip(kept, copies))]
    mapped = None
    for chunk in range(CHUNKS):
        for part in loads[chunk]:
            part.wait()
        cells = pl.ds(chunk * CELLS // CHUNKS, CELLS // CHUNKS)
        term = jnp.dot(field_ref[:, cells], spatial_ref[cells, :], preferred_element_type=jnp.float32)
        mapped = term if mapped is None else mapped + term
    loads[CHUNKS][0].wait()
    for keep in keeps:
        keep.start()
    upper = mapped.astype(jnp.bfloat16)
    lower = (mapped - upper.astype(jnp.float32)).astype(jnp.bfloat16)
    spectra = jnp.dot(
        time_ref[...], jnp.concatenate([upper, upper, lower], axis=0), preferred_element_type=jnp.float32
    )
    half = rows // 2
    lane = lax.broadcasted_iota(jnp.int32, (half, EDGE), 1)
    for band in range(bands):
        block = spectra[band * rows : (band + 1) * rows]
        send[band, 0:rows, :] = block[:, 0:COARSE].astype(jnp.bfloat16)
        send[band, rows : 2 * rows, :] = block[:, COARSE : COARSE + EDGE].astype(jnp.bfloat16)
        pairs = block[:, COARSE + EDGE :]
        if packed:
            pairs = jnp.where(lane < PAIRS, pairs[:half], pairs[half:])
        send[band, 2 * rows :, :] = pairs.astype(jnp.bfloat16)

    pl.semaphore_wait(barrier, nz * nf * 2 - 1)

    mine = my_c * nf + my_f

    def copy(first, dz, where, z, f, c, source_z, source):
        return pltpu.make_async_remote_copy(
            src_ref=send.at[f * 2 + c, pl.ds(first, last - first), :],
            dst_ref=out_ref.at[source_z, source, pl.ds(first, last - first), :],
            send_sem=send_sem.at[dz, where],
            recv_sem=recv_sem.at[source_z, source],
            device_id=(group, z, f, c),
            device_id_type=MESH,
        )

    def start(near, dz, where, z, f, c):
        if near:
            copy(0, dz, where, z, f, c, my_z, mine).start()
        else:
            @pl.when(my_c == 1)
            def _():
                copy(0, dz, where, z, f, c, my_z, mine).start()

            @pl.when(my_c == 0)
            def _():
                copy(rows, dz, where, z, f, c, my_z, mine).start()

    each_peer(start)
    own = pltpu.make_async_copy(send.at[my_f * 2 + my_c], out_ref.at[my_z, mine], own_sem)
    own.start()

    def finish(near, dz, where, z, f, c):
        if near:
            copy(0, dz, where, z, f, c, my_z, mine).wait_send()
            copy(0, dz, where, z, f, c, z, c * nf + f).wait_recv()
        else:
            for core, first in ((1, 0), (0, rows)):
                @pl.when(my_c == core)
                def _():
                    copy(first, dz, where, z, f, c, my_z, mine).wait_send()

                @pl.when(c == core)
                def _():
                    copy(first, dz, where, z, f, c, z, c * nf + f).wait_recv()

    own.wait()
    for keep in keeps:
        keep.wait()
    each_peer(finish)


def dot_nt(left, right):
    return lax.dot_general(left, right, (((1,), (1,)), ((), ())), preferred_element_type=jnp.float32)


def cross_kernel(
    nz, nf, rows, packed, scale,
    slots_ref, near_ref, code_ref, pair_ref, got_ref, table_ref, out_ref,
    where_ref, outer, rims, pairs, stage, sems,
):
    lanes = 2 * nf * rows
    half = rows // 2
    per_band = SEGLEN // 2 // (2 * nf)
    me = lax.axis_index("tiles")

    def place(slot):
        where_ref[slots_ref[slot]] = slot

    repeat(nz, place)

    def spread(slot):
        flat = got_ref[slot, :, rows : 2 * rows, :].reshape(lanes, EDGE)
        coded = dot_nt(table_ref[0 : 2 * EDGE, :], flat)
        outer[pl.ds(slot * 8, 8)] = coded.reshape(8, SIDE, lanes).astype(jnp.bfloat16)

    repeat(nz, spread)

    def entry(slot, edge):
        return where_ref[near_ref[slot, edge]] * 8 + code_ref[slot, edge]

    lane = lax.broadcasted_iota(jnp.int32, (1, EDGE), 1)

    def unpack(block):
        low = jnp.where(lane < PAIRS, block, jnp.zeros_like(block))
        if packed:
            return jnp.concatenate([low, jnp.where(lane < PAIRS, jnp.zeros_like(block), block)], axis=0)
        return low

    def sweep(slot):
        for edge in range(4):
            rims[slot, edge * SIDE : (edge + 1) * SIDE, :] = outer[entry(slot, edge)]
        own = jnp.concatenate([unpack(got_ref[slot, s, 2 * rows :, :]) for s in range(2 * nf)], axis=0)
        total = dot_nt(table_ref[256:384, :], own)
        total = total + jnp.dot(table_ref[384:512, :], rims[slot], preferred_element_type=jnp.float32)
        pairs[pl.ds(slot * 8, 8)] = total.reshape(8, SIDE // 2, lanes).astype(jnp.bfloat16)

    repeat(nz, sweep)

    def spectrum(slot):
        flat = got_ref[slot, :, 0:rows, :].reshape(lanes, COARSE)
        beyond = jnp.concatenate([pairs[entry(slot, edge)] for edge in range(4)], axis=0)
        total = dot_nt(table_ref[768:896, :], flat)
        total = total + jnp.dot(table_ref[512:640, :], rims[slot], preferred_element_type=jnp.float32)
        total = total + jnp.dot(table_ref[640:768, 0:PAIRS], beyond, preferred_element_type=jnp.float32)
        return total

    at = lax.broadcasted_iota(jnp.int32, (COARSE, lanes), 1)
    velocity = at >= lanes // 2
    height = spectrum(me).astype(jnp.bfloat16).astype(jnp.float32)
    height = jnp.where(velocity, pltpu.roll(height, lanes // 2, 1), 0.0)
    real_lane = at % rows < half
    turned = jnp.where(real_lane, pltpu.roll(height, lanes - half, 1), -pltpu.roll(height, half, 1))
    both = jnp.concatenate([height, turned], axis=0).astype(jnp.bfloat16)
    at_both = lax.broadcasted_iota(jnp.int32, (2 * COARSE, lanes), 1) % per_band
    for k in range(2):
        total = spectrum(where_ref[pair_ref[0, k]])
        partner = jnp.where(velocity, total, 0.0).astype(jnp.bfloat16)
        for f in range(per_band):
            chosen = jnp.where(at_both == f, both, jnp.zeros_like(both))
            cross = dot_nt(chosen, partner) * scale
            for o in range(2):
                stage[k, o, f] = cross[o * COARSE : (o + 1) * COARSE]
            if f % 4 == 3:
                part = (k, slice(None), pl.ds(f - 3, 4))
                pltpu.make_async_copy(stage.at[part], out_ref.at[(0, *part)], sems.at[k, f // 4]).start()
    for k in range(2):
        for f in range(0, per_band, 4):
            part = (k, slice(None), pl.ds(f, 4))
            pltpu.make_async_copy(stage.at[part], out_ref.at[(0, *part)], sems.at[k, f // 4]).wait()


def shards(nz, nf, fields, slot_tile_ids, neighbour_tile_ids, neighbour_rotation_code, paired_tile_ids):
    samples = fields.shape[2]
    segments = samples // SEGLEN
    bands = 2 * nf
    per_band = SEGLEN // 2 // bands
    rows = 2 * segments * per_band
    lanes = bands * rows
    packed = rows % 32 == 0
    height = 2 * rows + (rows // 2 if packed else rows)
    sender, receiver = spatial_tables()
    times = time_table(segments, bands)
    scale = float(1.0 / (segments * nf * np.sum(hann() ** 2)))
    vmem = pl.BlockSpec(memory_space=pltpu.VMEM)
    smem = pl.BlockSpec(memory_space=pltpu.SMEM)
    hbm = pl.BlockSpec(memory_space=pltpu.HBM)
    anywhere = pl.BlockSpec(memory_space=pl.ANY)
    ids = (slot_tile_ids, neighbour_tile_ids, neighbour_rotation_code, paired_tile_ids)
    kept = ids + (jnp.asarray(receiver),)
    got, *kept = pl.pallas_call(
        functools.partial(exchange_kernel, nz, nf, rows, packed),
        out_shape=[jax.ShapeDtypeStruct((nz, bands, height, EDGE), jnp.bfloat16)]
        + [jax.ShapeDtypeStruct(a.shape, a.dtype) for a in kept],
        in_specs=[hbm] * 8,
        out_specs=[anywhere] * 6,
        scratch_shapes=[
            pltpu.VMEM((samples, CELLS), jnp.bfloat16),
            pltpu.VMEM(sender.shape, jnp.bfloat16),
            pltpu.VMEM(times.shape, jnp.bfloat16),
            pltpu.VMEM((bands, height, EDGE), jnp.bfloat16),
            pltpu.SemaphoreType.DMA((nz, bands)),
            pltpu.SemaphoreType.DMA((nz, bands)),
            pltpu.SemaphoreType.DMA((2 * CHUNKS + 1,)),
            pltpu.SemaphoreType.DMA,
            pltpu.SemaphoreType.DMA((5,)),
        ],
        compiler_params=pltpu.CompilerParams(
            collective_id=0, has_side_effects=True, vmem_limit_bytes=4 << 20
        ),
        name="exchange",
    )(*[pltpu.with_memory_space_constraint(a, pltpu.HBM) for a in
         (fields.reshape(samples, CELLS), jnp.asarray(sender), jnp.asarray(times), *kept)])
    return pl.pallas_call(
        functools.partial(cross_kernel, nz, nf, rows, packed, scale),
        out_shape=jax.ShapeDtypeStruct((1, 2, 2, per_band, COARSE, COARSE), jnp.float32),
        in_specs=[smem, smem, smem, smem, vmem, vmem],
        out_specs=anywhere,
        scratch_shapes=[
            pltpu.SMEM((nz,), jnp.int32),
            pltpu.VMEM((nz * 8, SIDE, lanes), jnp.bfloat16),
            pltpu.VMEM((nz, EDGE, lanes), jnp.bfloat16),
            pltpu.VMEM((nz * 8, SIDE // 2, lanes), jnp.bfloat16),
            pltpu.VMEM((2, 2, per_band, COARSE, COARSE), jnp.float32),
            pltpu.SemaphoreType.DMA((2, per_band // 4)),
        ],
        compiler_params=pltpu.CompilerParams(vmem_limit_bytes=max(8, nz) << 20),
        name="cross",
    )(*kept[:4], got, kept[4])


def solution(mesh):
    placed = (P("field", "tiles", ("groups", "freq"), None), P(), P(), P(), P("tiles", None))
    return jax.shard_map(
        functools.partial(shards, mesh.shape["tiles"], mesh.shape["freq"]),
        mesh=mesh,
        in_specs=placed,
        out_specs=P(("groups", "tiles"), None, None, ("freq", "field"), None, None),
        check_vma=False,
    )
```
